32 devices in a mesh: row: 8 (over y, x, core), col: 4 (over z).
Axes of the slice: x: 2, y: 2, z: 4, core: 2. Of those that a mesh axis runs over, the one named last changes fastest.
Arguments:
- attn_out: bfloat16 [2, 256, 16384], P(None, 'row', 'col'), may hold values from -6 to 6
- o_weight: bfloat16 [16384, 16384], P('col', 'row'), may hold values from -0.046875 to 0.046875
- residual: float32 [2, 256, 16384], P(None, 'col', 'row'), may hold values from -73 to 73
- norm_gain: float32 [16384], replicated, may hold values from 0.5 to 1.5
- gram_in: float32 [16384, 16384], P('row', 'col'), may hold values from -0.1 to 1.5
Outputs:
- gram: float32 [16384, 16384], P('row', 'col')
The draws below stay inside these ranges and needn't reach their ends.
All inputs are finite; a program needn't handle non-finite values.
Results may differ from the reference program's by a relative error of at most 0.0003.
Values may be sent and summed in bfloat16 or wider, within the bound.
A program may use at most 192 MiB of HBM per device.

```python
import math
import jax
import jax.numpy as jnp
from jax import lax

D = 16384
GROUPS = 2
CT = 256


def draw_residual(key, part):
    subkeys = jax.random.split(key, 4)
    feature_ramp = jnp.exp(math.log(3.0) * jnp.arange(D, dtype=jnp.float32) / D)
    feature_rough = jnp.exp(jax.random.uniform(subkeys[0], (D,), jnp.float32, -0.69, 0.69))
    token_scale = jnp.exp(jax.random.uniform(subkeys[1], (GROUPS, CT, 1), jnp.float32, math.log(0.3), math.log(3.0)))
    entries = jnp.clip(jax.random.normal(subkeys[3], (GROUPS, CT, D), jnp.float32), -4.0, 4.0)
    return entries * token_scale * (feature_ramp * feature_rough)[None, None, :]


def draw_gram_in(key, part):
    subkeys = jax.random.split(jax.random.fold_in(key, 7), 2)
    diag_values = jax.random.uniform(subkeys[0], (D,), jnp.float32, 0.5, 1.5)
    off_values = jnp.clip(0.02 * jax.random.normal(subkeys[1], (D, D), jnp.float32), -0.1, 0.1)
    row_ids = jnp.arange(D, dtype=jnp.int32)
    on_diag = row_ids[:, None] == row_ids[None, :]
    return jnp.where(on_diag, diag_values[:, None], off_values)


def levels(rng, extent, shards, smallest, largest):
    def one(position, blocks):
        heights = jax.random.uniform(jax.random.fold_in(jax.random.fold_in(rng, 6), position), (blocks,), jnp.float32, smallest / len(shards), largest / len(shards))
        return jnp.repeat(jnp.exp(heights), extent[position] // blocks).reshape((-1,) + (1,) * (len(extent) - position - 1))

    loudness = one(*shards[0])
    for cut in shards[1:]:
        loudness = loudness * one(*cut)
    return loudness


def normal_values(stream_key, shape, scale, limit, cuts=(), held_as=jnp.bfloat16):
    level = levels(stream_key, shape, cuts, -0.22, 0.18) if cuts else 1.0
    values = jax.random.normal(stream_key, shape, jnp.float32) * scale * level
    return jnp.minimum(jnp.maximum(values, -limit), limit).astype(held_as)


def setup_inputs(seed: int = 0) -> dict:
    splits = jax.random.split(jax.random.key(seed), 6)
    attn_out = normal_values(splits[0], (GROUPS, CT, D), 1.0, 6.0, ((1, 8), (2, 4)))
    o_weight = normal_values(splits[1], (D, D), D ** -0.5, 0.046875, ((0, 4), (1, 8)))
    residual = draw_residual(jax.random.fold_in(splits[5], 71), 0)
    norm_gain = jnp.clip(1.0 + 0.1 * jax.random.normal(splits[3], (D,), jnp.float32), 0.5, 1.5)
    gram_in = draw_gram_in(jax.random.fold_in(splits[5], 71), 0)
    return {"attn_out": attn_out, "o_weight": o_weight, "residual": residual, "norm_gain": norm_gain, "gram_in": gram_in}


epsilon_norm = 1e-05
highest = lax.Precision.HIGHEST

def reference(attn_out, o_weight, residual, norm_gain, gram_in):
    weight_wide = o_weight.astype(jnp.float32)
    gram_sum = jnp.zeros((D, D), jnp.float32)
    for block_index in range(GROUPS):
        projected = jnp.dot(attn_out[block_index].astype(jnp.float32), weight_wide, precision=highest, preferred_element_type=jnp.float32)
        stream = projected + residual[block_index]
        mean_square = lax.optimization_barrier(jnp.mean(stream * stream, axis=1, keepdims=True))
        normed = stream * lax.rsqrt(mean_square + epsilon_norm) * norm_gain[None, :]
        gram_sum = gram_sum + lax.dot_general(normed, normed, (((0,), (0,)), ((), ())), precision=highest, preferred_element_type=jnp.float32)
    return gram_in + gram_sum / (GROUPS * CT)
```

```python
import functools

import jax
import jax.numpy as jnp
from jax import lax
from jax.experimental import pallas as pl
from jax.experimental.pallas import tpu as pltpu
from jax.sharding import PartitionSpec as P

epsilon_norm = 1e-05
highest = lax.Precision.HIGHEST
MESH = pl.DeviceIdType.MESH
LOG_TOP = 8.4


def power15(v):
    v2 = v * v
    v3 = v2 * v
    v5 = v3 * v2
    return v5 * v5 * v5


def root15(y):
    y = y.astype(jnp.float32)
    mag = jnp.abs(y)
    safe = jnp.maximum(mag, 1e-37)
    root = jnp.exp2(jnp.log2(safe) * (1.0 / 15.0))
    return jnp.where(mag < 1.5e-37, 0.0, jnp.where(y < 0, -root, root))


def remote(src, dst, send_sem, recv_sem, row, col):
    return pltpu.make_async_remote_copy(
        src_ref=src, dst_ref=dst, send_sem=send_sem, recv_sem=recv_sem,
        device_id=(row, col), device_id_type=MESH)


def gather_kernel(rows, fan, own_ref, out_ref, local_sem, send_sem, fwd_sem, recv_sem):
    me = lax.axis_index("row")
    col = lax.axis_index("col")
    chips = rows // fan
    chip, core = me // fan, me % fan
    barrier = pltpu.get_barrier_semaphore()
    for off in range(1, rows):
        pl.semaphore_signal(barrier, inc=1, device_id=((me + off) % rows, col), device_id_type=MESH)
    pl.semaphore_wait(barrier, rows - 1)
    pending = []
    local = pltpu.make_async_copy(own_ref, out_ref.at[me], local_sem)
    local.start()
    for off in range(1, chips):
        there = ((chip + off) % chips) * fan + core
        copy = remote(own_ref, out_ref.at[me], send_sem.at[off], recv_sem.at[me], there, col)
        copy.start()
        pending.append(copy)
    for other in range(1, fan):
        mate = chip * fan + (core + other) % fan
        copy = remote(own_ref, out_ref.at[me], fwd_sem.at[0, other], recv_sem.at[me], mate, col)
        copy.start()
        pending.append(copy)
    for off in range(1, chips):
        slot = ((chip + chips - off) % chips) * fan + core
        remote(own_ref, out_ref.at[slot], send_sem.at[off], recv_sem.at[slot], me, col).wait_recv()
        for other in range(1, fan):
            mate = chip * fan + (core + other) % fan
            copy = remote(out_ref.at[slot], out_ref.at[slot], fwd_sem.at[off, other], recv_sem.at[slot], mate, col)
            copy.start()
            pending.append(copy)
    for off in range(chips):
        for other in range(1, fan):
            slot = ((chip + chips - off) % chips) * fan + (core + other) % fan
            remote(own_ref, out_ref.at[slot], fwd_sem.at[off, other], recv_sem.at[slot], me, col).wait_recv()
    for copy in pending:
        copy.wait_send()
    local.wait()


def gather_rows(own, rows, fan):
    chips = rows // fan
    return pl.pallas_call(
        functools.partial(gather_kernel, rows, fan),
        out_shape=jax.ShapeDtypeStruct((rows,) + own.shape, own.dtype),
        in_specs=[pl.BlockSpec(memory_space=pltpu.VMEM)],
        out_specs=pl.BlockSpec(memory_space=pltpu.VMEM),
        scratch_shapes=[
            pltpu.SemaphoreType.DMA,
            pltpu.SemaphoreType.DMA((chips,)),
            pltpu.SemaphoreType.DMA((chips, fan)),
            pltpu.SemaphoreType.DMA((rows,)),
        ],
        compiler_params=pltpu.CompilerParams(collective_id=0, has_side_effects=True, vmem_limit_bytes=40 << 20),
        name="gather_rows",
    )(own)


def panel_kernel(rows, cols, fan, part_ref, rp_ref, cp_ref, sums, stat_own, stats,
                 rs_send, rs_recv, st_send, st_recv, ag_send, ag_recv, ring_send, mate_send, cp_recv, loc_sem):
    me = lax.axis_index("row")
    col = lax.axis_index("col")
    chips = rows // fan
    chip, core = me // fan, me % fan
    tokens, width = part_ref.shape
    half = tokens // 2
    model = width * rows
    last = cols - 1
    order = [j ^ (j >> 1) for j in range(chips)]
    ahead = jnp.int32(0)
    behind = jnp.int32(0)
    for j in range(chips):
        ahead = jnp.where(chip == order[j], order[(j + 1) % chips], ahead)
        behind = jnp.where(chip == order[j], order[(j + chips - 1) % chips], behind)
    to_chip = jnp.where(core % 2 == 0, ahead, behind)
    to_row = to_chip * fan + core
    is_source = chip == col
    feeds_ring = to_chip != col

    barrier = pltpu.get_barrier_semaphore()
    for off in range(1, rows):
        pl.semaphore_signal(barrier, inc=1, device_id=((me + off) % rows, col), device_id_type=MESH)

    @pl.when(col > 0)
    def _():
        pl.semaphore_signal(barrier, inc=1, device_id=(me, col - 1), device_id_type=MESH)

    @pl.when(col < last)
    def _():
        pl.semaphore_signal(barrier, inc=1, device_id=(me, col + 1), device_id_type=MESH)

    pl.semaphore_wait(barrier, rows - 1 + jnp.minimum(col, 1) + jnp.minimum(last - col, 1))

    rs_count = rs_send.shape[1]
    rs_rows = half // rs_count

    def rs_copy(d, i, src):
        here = pl.ds(pl.multiple_of(i * rs_rows, rs_rows), rs_rows)
        nxt = jnp.maximum(col - 1, 0) if d == 0 else jnp.minimum(col + 1, last)
        source = part_ref.at[pl.ds(pl.multiple_of(d * half + i * rs_rows, rs_rows), rs_rows)] if src == "part" else sums.at[d, here]
        return remote(source, sums.at[d, here], rs_send.at[d, i], rs_recv.at[d, i], me, nxt)

    def rs_step(i, carry):
        for d in range(2):
            first = last if d == 0 else 0
            end = last - first

            @pl.when(col == first)
            def _(d=d):
                rs_copy(d, i, "part").start()

            @pl.when(col != first)
            def _(d=d, end=end):
                rs_copy(d, i, "sums").wait_recv()
                here = pl.ds(pl.multiple_of(i * rs_rows, rs_rows), rs_rows)
                mine = pl.ds(pl.multiple_of(d * half + i * rs_rows, rs_rows), rs_rows)
                sums[d, here, :] = sums[d, here, :] + part_ref[mine, :]

                @pl.when(col != end)
                def _():
                    rs_copy(d, i, "sums").start()
        return carry

    lax.fori_loop(0, rs_count, rs_step, 0)

    block = 128
    for d in range(2):
        end = 0 if d == 0 else last

        @pl.when(col == end)
        def _(d=d):
            ones = jnp.ones((8, width), jnp.float32)
            for b in range(half // block):
                x = sums[d, b * block:(b + 1) * block, :]
                stat_own[:, b * block:(b + 1) * block] = lax.dot_general(
                    ones, x * x, (((1,), (1,)), ((), ())), precision=highest, preferred_element_type=jnp.float32)
            for off in range(1, rows):
                remote(stat_own, stats.at[off], st_send.at[off], st_recv.at[off], (me + off) % rows, col).start()
            total = stat_own[...]
            for off in range(1, rows):
                remote(stat_own, stats.at[off], st_send.at[off], st_recv.at[off], (me + off) % rows, col).wait_recv()
                total = total + stats[off]
            inverse = lax.rsqrt(total / model + epsilon_norm) * (2.0 ** LOG_TOP / model ** 0.5)
            spread = jnp.full((8, 128), 0.125, jnp.float32)
            for b in range(half // block):
                scale = lax.dot_general(
                    inverse[:, b * block:(b + 1) * block], spread, (((0,), (0,)), ((), ())),
                    precision=highest, preferred_element_type=jnp.float32)

                def code(j, carry, b=b, scale=scale):
                    lanes = pl.ds(pl.multiple_of(j * 128, 128), 128)
                    v = sums[d, b * block:(b + 1) * block, lanes] * scale
                    rp_ref[d * half + b * block:d * half + (b + 1) * block, lanes] = power15(v).astype(jnp.bfloat16)
                    return carry

                lax.fori_loop(0, width // 128, code, 0)
            for off in range(1, rows):
                remote(stat_own, stats.at[off], st_send.at[off], st_recv.at[off], (me + off) % rows, col).wait_send()

    ag_count = ag_send.shape[1]
    ag_rows = half // ag_count

    def span(d, i):
        return pl.ds(pl.multiple_of(d * half + i * ag_rows, ag_rows), ag_rows)

    def ag_copy(d, i):
        nxt = jnp.minimum(col + 1, last) if d == 0 else jnp.maximum(col - 1, 0)
        return remote(rp_ref.at[span(d, i)], rp_ref.at[span(d, i)], ag_send.at[d, i], ag_recv.at[d, i], me, nxt)

    def ring_copy(d, i, from_row):
        src = rp_ref.at[span(d, i)] if from_row else cp_ref.at[core, span(d, i)]
        return remote(src, cp_ref.at[core, span(d, i)], ring_send.at[d, i], cp_recv.at[core, d, i], to_row, col)

    def mate_copy(d, i, other, from_row):
        mate = chip * fan + (core + other) % fan
        src = rp_ref.at[span(d, i)] if from_row else cp_ref.at[core, span(d, i)]
        return remote(src, cp_ref.at[core, span(d, i)], mate_send.at[other, d, i], cp_recv.at[core, d, i], mate, col)

    def local_copy(d, i):
        return pltpu.make_async_copy(rp_ref.at[span(d, i)], cp_ref.at[core, span(d, i)], loc_sem.at[d, i])

    def ag_step(i):
        for d in range(2):
            first = 0 if d == 0 else last
            end = last - first

            @pl.when(col != first)
            def _(d=d):
                ag_copy(d, i).wait_recv()

            @pl.when(col != end)
            def _(d=d):
                ag_copy(d, i).start()

            @pl.when(is_source)
            def _(d=d):
                ring_copy(d, i, True).start()
                local_copy(d, i).start()
                for other in range(1, fan):
                    mate_copy(d, i, other, True).start()

    def ring_step(i):
        for d in range(2):
            @pl.when(jnp.logical_not(is_source))
            def _(d=d):
                ring_copy(d, i, False).wait_recv()

                @pl.when(feeds_ring)
                def _():
                    ring_copy(d, i, False).start()

                for other in range(1, fan):
                    mate_copy(d, i, other, False).start()

    lag = min(2, ag_count)
    for i in range(ag_count + lag):
        if i < ag_count:
            ag_step(i)
        if i >= lag:
            ring_step(i - lag)

    def drain(i, carry):
        for d in range(2):
            rs_first = last if d == 0 else 0
            ag_first = last - rs_first

            @pl.when(col != rs_first)
            def _(d=d):
                pass

            for other in range(1, fan):
                theirs = (core + other) % fan
                remote(rp_ref.at[span(d, i)], cp_ref.at[theirs, span(d, i)], mate_send.at[other, d, i],
                       cp_recv.at[theirs, d, i], me, col).wait_recv()
                mate_copy(d, i, other, True).wait_send()

            @pl.when(col != last - ag_first)
            def _(d=d):
                ag_copy(d, i).wait_send()

            @pl.when(is_source)
            def _(d=d):
                local_copy(d, i).wait()

            @pl.when(jnp.logical_or(is_source, feeds_ring))
            def _(d=d):
                ring_copy(d, i, True).wait_send()
        return carry

    lax.fori_loop(0, ag_count, drain, 0)

    def rs_drain(i, carry):
        for d in range(2):
            end = 0 if d == 0 else last

            @pl.when(col != end)
            def _(d=d):
                rs_copy(d, i, "sums").wait_send()
        return carry

    lax.fori_loop(0, rs_count, rs_drain, 0)


def panels(part, rows, cols, fan):
    tokens, width = part.shape
    half = tokens // 2
    rs_count = half // 16
    ag_count = half // 32
    vmem = pl.BlockSpec(memory_space=pltpu.VMEM)
    dma = pltpu.SemaphoreType.DMA
    return pl.pallas_call(
        functools.partial(panel_kernel, rows, cols, fan),
        out_shape=(
            jax.ShapeDtypeStruct((tokens, width), jnp.bfloat16),
            jax.ShapeDtypeStruct((fan, tokens, width), jnp.bfloat16),
        ),
        in_specs=[vmem],
        out_specs=(vmem, vmem),
        scratch_shapes=[
            pltpu.VMEM((2, half, width), jnp.float32),
            pltpu.VMEM((8, half), jnp.float32),
            pltpu.VMEM((rows, 8, half), jnp.float32),
            dma((2, rs_count)), dma((2, rs_count)),
            dma((rows,)), dma((rows,)),
            dma((2, ag_count)), dma((2, ag_count)),
            dma((2, ag_count)), dma((fan, 2, ag_count)), dma((fan, 2, ag_count)),
            dma((2, ag_count)),
        ],
        compiler_params=pltpu.CompilerParams(collective_id=1, has_side_effects=True, vmem_limit_bytes=48 << 20),
        name="panels",
    )(part)


def split(value):
    high = lax.reduce_precision(value, 8, 7)
    low = value - high
    return high.astype(jnp.bfloat16), low.astype(jnp.bfloat16)


def body(attn_out, o_weight, residual, norm_gain, gram_in):
    rows = lax.axis_size("row")
    cols = lax.axis_size("col")
    fan = rows // cols
    row_index = lax.axis_index("row")
    col_index = lax.axis_index("col")
    groups, tile = attn_out.shape[0], attn_out.shape[1]
    width, model_width = o_weight.shape[1], o_weight.shape[1] * rows
    tokens = groups * tile * rows

    attn = gather_rows(attn_out.reshape(groups * tile, -1), rows, fan).reshape(tokens, -1)
    part = jnp.dot(attn, o_weight, preferred_element_type=jnp.float32)
    mine = residual.reshape(groups, fan, tile, width).transpose(1, 0, 2, 3).reshape(-1, width)
    offset = col_index * mine.shape[0]
    own = lax.dynamic_slice_in_dim(part, offset, mine.shape[0], 0) + mine
    part = lax.dynamic_update_slice_in_dim(part, own, offset, 0)
    row_code, col_code = panels(part, rows, cols, fan)

    unit = model_width ** 0.5 / 2.0 ** LOG_TOP
    gain_rows = lax.dynamic_slice_in_dim(norm_gain, row_index * width, width) * (unit / tokens)
    gain_cols = (lax.dynamic_slice_in_dim(norm_gain, col_index * fan * width, fan * width) * unit).reshape(fan, 1, width)
    lh, ll = split(root15(row_code) * gain_rows[None, :])
    rh, rl = split(root15(col_code) * gain_cols)
    left = jnp.concatenate([lh, lh, ll], axis=0)
    right = jnp.concatenate([rh, rl, rh], axis=1)
    gram = lax.dot_general(
        left, right.transpose(1, 0, 2).reshape(3 * tokens, fan * width), (((0,), (0,)), ((), ())),
        preferred_element_type=jnp.float32)
    return gram_in + gram


def solution(mesh):
    return jax.shard_map(
        body,
        mesh=mesh,
        in_specs=(
            P(None, "row", "col"),
            P("col", "row"),
            P(None, "col", "row"),
            P(),
            P("row", "col"),
        ),
        out_specs=P("row", "col"),
        check_vma=False,
    )
```

```python
import functools

import jax
import jax.numpy as jnp
from jax import lax
from jax.experimental import pallas as pl
from jax.experimental.pallas import tpu as pltpu
from jax.sharding import PartitionSpec as P

epsilon_norm = 1e-05
highest = lax.Precision.HIGHEST
MESH = pl.DeviceIdType.MESH
LOG_TOP = 8.4


def power15(v):
    v2 = v * v
    v3 = v2 * v
    v5 = v3 * v2
    return v5 * v5 * v5


def root15(y):
    y = y.astype(jnp.float32)
    mag = jnp.abs(y)
    safe = jnp.maximum(mag, 1e-37)
    root = jnp.exp2(jnp.log2(safe) * (1.0 / 15.0))
    return jnp.where(mag < 1.5e-37, 0.0, jnp.where(y < 0, -root, root))


def remote(src, dst, send_sem, recv_sem, row, col):
    return pltpu.make_async_remote_copy(
        src_ref=src, dst_ref=dst, send_sem=send_sem, recv_sem=recv_sem,
        device_id=(row, col), device_id_type=MESH)


def gather_kernel(rows, fan, own_ref, out_ref, local_sem, send_sem, fwd_sem, recv_sem):
    me = lax.axis_index("row")
    col = lax.axis_index("col")
    chips = rows // fan
    chip, core = me // fan, me % fan
    barrier = pltpu.get_barrier_semaphore()
    for off in range(1, rows):
        pl.semaphore_signal(barrier, inc=1, device_id=((me + off) % rows, col), device_id_type=MESH)
    pl.semaphore_wait(barrier, rows - 1)
    pending = []
    local = pltpu.make_async_copy(own_ref, out_ref.at[me], local_sem)
    local.start()
    for off in range(1, chips):
        there = ((chip + off) % chips) * fan + core
        copy = remote(own_ref, out_ref.at[me], send_sem.at[off], recv_sem.at[me], there, col)
        copy.start()
        pending.append(copy)
    for other in range(1, fan):
        mate = chip * fan + (core + other) % fan
        copy = remote(own_ref, out_ref.at[me], fwd_sem.at[0, other], recv_sem.at[me], mate, col)
        copy.start()
        pending.append(copy)
    for off in range(1, chips):
        slot = ((chip + chips - off) % chips) * fan + core
        remote(own_ref, out_ref.at[slot], send_sem.at[off], recv_sem.at[slot], me, col).wait_recv()
        for other in range(1, fan):
            mate = chip * fan + (core + other) % fan
            copy = remote(out_ref.at[slot], out_ref.at[slot], fwd_sem.at[off, other], recv_sem.at[slot], mate, col)
            copy.start()
            pending.append(copy)
    for off in range(chips):
        for other in range(1, fan):
            slot = ((chip + chips - off) % chips) * fan + (core + other) % fan
            remote(own_ref, out_ref.at[slot], fwd_sem.at[off, other], recv_sem.at[slot], me, col).wait_recv()
    for copy in pending:
        copy.wait_send()
    local.wait()


def gather_rows(own, rows, fan):
    chips = rows // fan
    return pl.pallas_call(
        functools.partial(gather_kernel, rows, fan),
        out_shape=jax.ShapeDtypeStruct((rows,) + own.shape, own.dtype),
        in_specs=[pl.BlockSpec(memory_space=pltpu.VMEM)],
        out_specs=pl.BlockSpec(memory_space=pltpu.VMEM),
        scratch_shapes=[
            pltpu.SemaphoreType.DMA,
            pltpu.SemaphoreType.DMA((chips,)),
            pltpu.SemaphoreType.DMA((chips, fan)),
            pltpu.SemaphoreType.DMA((rows,)),
        ],
        compiler_params=pltpu.CompilerParams(collective_id=0, has_side_effects=True, vmem_limit_bytes=40 << 20),
        name="gather_rows",
    )(own)


def panel_kernel(rows, cols, fan, part_ref, rp_ref, cp_ref, sums, stat_own, stats,
                 rs_send, rs_recv, st_send, st_recv, ag_send, ag_recv, ring_send, mate_send, cp_recv, loc_sem):
    me = lax.axis_index("row")
    col = lax.axis_index("col")
    chips = rows // fan
    chip, core = me // fan, me % fan
    tokens, width = part_ref.shape
    half = tokens // 2
    model = width * rows
    last = cols - 1
    order = [j ^ (j >> 1) for j in range(chips)]
    ahead = jnp.int32(0)
    behind = jnp.int32(0)
    spot = jnp.int32(0)
    source_spot = jnp.int32(0)
    for j in range(chips):
        spot = jnp.where(chip == order[j], j, spot)
        source_spot = jnp.where(col == order[j], j, source_spot)
        ahead = jnp.where(chip == order[j], order[(j + 1) % chips], ahead)
        behind = jnp.where(chip == order[j], order[(j + chips - 1) % chips], behind)
    to_chip = jnp.where(core % 2 == 0, ahead, behind)
    to_row = to_chip * fan + core
    is_source = chip == col
    feeds_ring = to_chip != col
    turn = jnp.where(core % 2 == 0, spot - source_spot, source_spot - spot)
    ring_hops = (turn + chips) % chips

    barrier = pltpu.get_barrier_semaphore()
    for off in range(1, rows):
        pl.semaphore_signal(barrier, inc=1, device_id=((me + off) % rows, col), device_id_type=MESH)

    @pl.when(col > 0)
    def _():
        pl.semaphore_signal(barrier, inc=1, device_id=(me, col - 1), device_id_type=MESH)

    @pl.when(col < last)
    def _():
        pl.semaphore_signal(barrier, inc=1, device_id=(me, col + 1), device_id_type=MESH)

    pl.semaphore_wait(barrier, rows - 1 + jnp.minimum(col, 1) + jnp.minimum(last - col, 1))

    rs_count = rs_send.shape[1]
    rs_rows = half // rs_count

    def rs_copy(d, i, src):
        here = pl.ds(pl.multiple_of(i * rs_rows, rs_rows), rs_rows)
        nxt = jnp.maximum(col - 1, 0) if d == 0 else jnp.minimum(col + 1, last)
        source = part_ref.at[pl.ds(pl.multiple_of(d * half + i * rs_rows, rs_rows), rs_rows)] if src == "part" else sums.at[d, here]
        return remote(source, sums.at[d, here], rs_send.at[d, i], rs_recv.at[d, i], me, nxt)

    for d in range(2):
        @pl.when(col == (last if d == 0 else 0))
        def _(d=d):
            def send_all(i, carry):
                rs_copy(d, i, "part").start()
                return carry

            lax.fori_loop(0, rs_count, send_all, 0)

    def rs_step(s, carry):
        for d in range(2):
            end = 0 if d == 0 else last
            hops = last - col if d == 0 else col
            i = s - hops

            @pl.when(jnp.logical_and(hops > 0, jnp.logical_and(i >= 0, i < rs_count)))
            def _(d=d, end=end, i=i):
                rs_copy(d, i, "sums").wait_recv()
                here = pl.ds(pl.multiple_of(i * rs_rows, rs_rows), rs_rows)
                mine = pl.ds(pl.multiple_of(d * half + i * rs_rows, rs_rows), rs_rows)
                sums[d, here, :] = sums[d, here, :] + part_ref[mine, :]

                @pl.when(col != end)
                def _():
                    rs_copy(d, i, "sums").start()
        return carry

    lax.fori_loop(1, rs_count + last, rs_step, 0)

    block = 128
    for d in range(2):
        end = 0 if d == 0 else last

        @pl.when(col == end)
        def _(d=d):
            ones = jnp.ones((8, width), jnp.float32)
            for b in range(half // block):
                x = sums[d, b * block:(b + 1) * block, :]
                stat_own[:, b * block:(b + 1) * block] = lax.dot_general(
                    ones, x * x, (((1,), (1,)), ((), ())), precision=highest, preferred_element_type=jnp.float32)
            for off in range(1, rows):
                remote(stat_own, stats.at[off], st_send.at[off], st_recv.at[off], (me + off) % rows, col).start()
            total = stat_own[...]
            for off in range(1, rows):
                remote(stat_own, stats.at[off], st_send.at[off], st_recv.at[off], (me + off) % rows, col).wait_recv()
                total = total + stats[off]
            inverse = lax.rsqrt(total / model + epsilon_norm) * (2.0 ** LOG_TOP / model ** 0.5)
            spread = jnp.full((8, 128), 0.125, jnp.float32)
            for b in range(half // block):
                scale = lax.dot_general(
                    inverse[:, b * block:(b + 1) * block], spread, (((0,), (0,)), ((), ())),
                    precision=highest, preferred_element_type=jnp.float32)

                def code(j, carry, b=b, scale=scale):
                    lanes = pl.ds(pl.multiple_of(j * 128, 128), 128)
                    v = sums[d, b * block:(b + 1) * block, lanes] * scale
                    rp_ref[d * half + b * block:d * half + (b + 1) * block, lanes] = power15(v).astype(jnp.bfloat16)
                    return carry

                lax.fori_loop(0, width // 128, code, 0)
            for off in range(1, rows):
                remote(stat_own, stats.at[off], st_send.at[off], st_recv.at[off], (me + off) % rows, col).wait_send()

    ag_count = ag_send.shape[1]
    ag_rows = half // ag_count

    def span(d, i):
        return pl.ds(pl.multiple_of(d * half + i * ag_rows, ag_rows), ag_rows)

    def lanes(which):
        return pl.ds(pl.multiple_of(which * width, width), width)

    def ag_copy(d, i):
        nxt = jnp.minimum(col + 1, last) if d == 0 else jnp.maximum(col - 1, 0)
        return remote(rp_ref.at[span(d, i)], rp_ref.at[span(d, i)], ag_send.at[d, i], ag_recv.at[d, i], me, nxt)

    def ring_copy(d, i, from_row):
        src = rp_ref.at[span(d, i)] if from_row else cp_ref.at[span(d, i), lanes(core)]
        return remote(src, cp_ref.at[span(d, i), lanes(core)], ring_send.at[d, i], cp_recv.at[core, d, i], to_row, col)

    def mate_copy(d, i, other, from_row):
        mate = chip * fan + (core + other) % fan
        src = rp_ref.at[span(d, i)] if from_row else cp_ref.at[span(d, i), lanes(core)]
        return remote(src, cp_ref.at[span(d, i), lanes(core)], mate_send.at[other, d, i], cp_recv.at[core, d, i], mate, col)

    def local_copy(d, i):
        return pltpu.make_async_copy(rp_ref.at[span(d, i)], cp_ref.at[span(d, i), lanes(core)], loc_sem.at[d, i])

    def have_panel(d, i):
        end = last if d == 0 else 0

        @pl.when(col != end)
        def _():
            ag_copy(d, i).start()

        @pl.when(is_source)
        def _():
            ring_copy(d, i, True).start()
            local_copy(d, i).start()
            for other in range(1, fan):
                mate_copy(d, i, other, True).start()

    for d in range(2):
        @pl.when(col == (0 if d == 0 else last))
        def _(d=d):
            def send_all(i, carry):
                have_panel(d, i)
                return carry

            lax.fori_loop(0, ag_count, send_all, 0)

    def ag_step(s, carry):
        for d in range(2):
            hops = col if d == 0 else last - col
            i = s - hops

            @pl.when(jnp.logical_and(hops > 0, jnp.logical_and(i >= 0, i < ag_count)))
            def _(d=d, i=i):
                ag_copy(d, i).wait_recv()
                have_panel(d, i)

        for d in range(2):
            hops = (col if d == 0 else last - col) + ring_hops
            i = s - hops

            @pl.when(jnp.logical_and(ring_hops > 0, jnp.logical_and(i >= 0, i < ag_count)))
            def _(d=d, i=i):
                ring_copy(d, i, False).wait_recv()

                @pl.when(feeds_ring)
                def _():
                    ring_copy(d, i, False).start()

                for other in range(1, fan):
                    mate_copy(d, i, other, False).start()
        return carry

    lax.fori_loop(1, ag_count + last + chips - 1, ag_step, 0)

    def drain(i, carry):
        for d in range(2):
            rs_first = last if d == 0 else 0
            ag_first = last - rs_first

            for other in range(1, fan):
                theirs = (core + other) % fan
                remote(rp_ref.at[span(d, i)], cp_ref.at[span(d, i), lanes(theirs)], mate_send.at[other, d, i],
                       cp_recv.at[theirs, d, i], me, col).wait_recv()
                mate_copy(d, i, other, True).wait_send()

            @pl.when(col != last - ag_first)
            def _(d=d):
                ag_copy(d, i).wait_send()

            @pl.when(is_source)
            def _(d=d):
                local_copy(d, i).wait()

            @pl.when(jnp.logical_or(is_source, feeds_ring))
            def _(d=d):
                ring_copy(d, i, True).wait_send()
        return carry

    lax.fori_loop(0, ag_count, drain, 0)

    def rs_drain(i, carry):
        for d in range(2):
            end = 0 if d == 0 else last

            @pl.when(col != end)
            def _(d=d):
                rs_copy(d, i, "sums").wait_send()
        return carry

    lax.fori_loop(0, rs_count, rs_drain, 0)


def panels(part, rows, cols, fan):
    tokens, width = part.shape
    half = tokens // 2
    rs_count = half // 16
    ag_count = half // 32
    vmem = pl.BlockSpec(memory_space=pltpu.VMEM)
    dma = pltpu.SemaphoreType.DMA
    return pl.pallas_call(
        functools.partial(panel_kernel, rows, cols, fan),
        out_shape=(
            jax.ShapeDtypeStruct((tokens, width), jnp.bfloat16),
            jax.ShapeDtypeStruct((tokens, fan * width), jnp.bfloat16),
        ),
        in_specs=[vmem],
        out_specs=(vmem, vmem),
        scratch_shapes=[
            pltpu.VMEM((2, half, width), jnp.float32),
            pltpu.VMEM((8, half), jnp.float32),
            pltpu.VMEM((rows, 8, half), jnp.float32),
            dma((2, rs_count)), dma((2, rs_count)),
            dma((rows,)), dma((rows,)),
            dma((2, ag_count)), dma((2, ag_count)),
            dma((2, ag_count)), dma((fan, 2, ag_count)), dma((fan, 2, ag_count)),
            dma((2, ag_count)),
        ],
        compiler_params=pltpu.CompilerParams(collective_id=1, has_side_effects=True, vmem_limit_bytes=48 << 20),
        name="panels",
    )(part)


def split(value):
    high = lax.reduce_precision(value, 8, 7)
    low = value - high
    return high.astype(jnp.bfloat16), low.astype(jnp.bfloat16)


def body(attn_out, o_weight, residual, norm_gain, gram_in):
    rows = lax.axis_size("row")
    cols = lax.axis_size("col")
    fan = rows // cols
    row_index = lax.axis_index("row")
    col_index = lax.axis_index("col")
    groups, tile = attn_out.shape[0], attn_out.shape[1]
    width, model_width = o_weight.shape[1], o_weight.shape[1] * rows
    tokens = groups * tile * rows

    attn = gather_rows(attn_out.reshape(groups * tile, -1), rows, fan).reshape(tokens, -1)
    part = jnp.dot(attn, o_weight, preferred_element_type=jnp.float32)
    mine = residual.reshape(groups, fan, tile, width).transpose(1, 0, 2, 3).reshape(-1, width)
    offset = col_index * mine.shape[0]
    own = lax.dynamic_slice_in_dim(part, offset, mine.shape[0], 0) + mine
    part = lax.dynamic_update_slice_in_dim(part, own, offset, 0)
    row_code, col_code = panels(part, rows, cols, fan)

    unit = model_width ** 0.5 / 2.0 ** LOG_TOP
    gain_rows = lax.dynamic_slice_in_dim(norm_gain, row_index * width, width) * (unit / tokens)
    gain_cols = (lax.dynamic_slice_in_dim(norm_gain, col_index * fan * width, fan * width) * unit)[None, :]
    lh, ll = split(root15(row_code) * gain_rows[None, :])
    rh, rl = split(root15(col_code) * gain_cols)
    left = jnp.concatenate([lh, lh, ll], axis=0)
    right = jnp.concatenate([rh, rl, rh], axis=0)
    gram = lax.dot_general(
        left, right, (((0,), (0,)), ((), ())),
        preferred_element_type=jnp.float32)
    return gram_in + gram


def solution(mesh):
    return jax.shard_map(
        body,
        mesh=mesh,
        in_specs=(
            P(None, "row", "col"),
            P("col", "row"),
            P(None, "col", "row"),
            P(),
            P("row", "col"),
        ),
        out_specs=P("row", "col"),
        check_vma=False,
    )
```
